128 devices in a mesh: ctx: 16 (over x_lo, y, core), fsdp: 8 (over z, x_hi).
Axes of the slice: x: 4 (x_hi: 2, x_lo: 2; x = x_hi * 2 + x_lo), y: 4, z: 4, core: 2. Of those that a mesh axis runs over, the one named last changes fastest.
Arguments:
- block_input: bfloat16 [8, 2, 1024, 1152], P('fsdp', None, 'ctx'), may hold values from -6 to 6
- doc_ids: int32 [8, 2, 1024], P('fsdp', None, 'ctx'), may hold values from 0 to 3, as said below
- positions: int32 [8, 2, 1024], P('fsdp', None, 'ctx'), may hold values from 0 to 1023
- qkv_weight: bfloat16 [1152, 1536], P('fsdp')
- out_weight: bfloat16 [1024, 1152], P('fsdp'), may hold values from -0.1875 to 0.1875
- gate_up_weight: bfloat16 [1152, 13824], P('fsdp'), may hold values from -0.1875 to 0.1875
- down_weight: bfloat16 [6912, 1152], P('fsdp'), may hold values from -0.078125 to 0.078125
- scale_attn_in: float32 [1152], replicated, may hold values from 0.1 to 1.9
- scale_attn_out: float32 [1152], replicated, may hold values from 0.1 to 1.9
- scale_ff_in: float32 [1152], replicated, may hold values from 0.1 to 1.9
- scale_ff_out: float32 [1152], replicated, may hold values from 0.1 to 1.9
- scale_query: float32 [256], replicated, may hold values from 0.5 to 4.5
- scale_key: float32 [256], replicated, may hold values from 0.5 to 4.5
- grad_output: bfloat16 [8, 2, 1024, 1152], P('fsdp', None, 'ctx'), may hold values from -6 to 6
Outputs:
- block_output: bfloat16 [8, 2, 1024, 1152], P('fsdp', None, 'ctx')
- input_grad: float32 [8, 2, 1024, 1152], P('fsdp', None, 'ctx')
- qkv_grad: float32 [1152, 1536], P(None, ('ctx', 'fsdp'))
- out_grad: float32 [1024, 1152], P(('ctx', 'fsdp'))
- gate_up_grad: float32 [1152, 13824], P(None, ('ctx', 'fsdp'))
- down_grad: float32 [6912, 1152], P(('ctx', 'fsdp'))
- attn_in_grad: float32 [1152], replicated
- attn_out_grad: float32 [1152], replicated
- ff_in_grad: float32 [1152], replicated
- ff_out_grad: float32 [1152], replicated
- query_gain_grad: float32 [256], replicated
- key_gain_grad: float32 [256], replicated
The draws below stay inside these ranges and needn't reach their ends.
Inputs may be any that keep to these rules, and one draw needn't show every extreme that they name: `doc_ids`: within each sequence document numbers start at 0 and never fall; a token's position is its distance from the first token of its document. The last sequence of each pair is one document; every other sequence holds exactly 4 documents.
All inputs are finite; a program needn't handle non-finite values.
Results may differ from the reference program's by a relative error of at most 0.02.
The reference program's roundings to bfloat16 on the way count: a program that leaves them out, or rounds other values in their place, can miss the bound.
Values may be sent and summed in bfloat16 or wider, within the bound.
A program may use at most 384 MiB of HBM per device.

```python
import math
import jax
import jax.numpy as jnp
from jax import lax

D = 1152
FF = 6912
HEADS = 4
HEAD_DIM = 256
SEQS = 2
LENGTH = 1024
GROUPS = 8


def doc_layout(key):
    layout_key = jax.random.fold_in(key, 4242)
    score_top = 2 ** 30 // LENGTH
    raw_scores = jax.random.randint(layout_key, (GROUPS, SEQS, LENGTH), 0, score_top)
    column_index = jnp.arange(LENGTH, dtype=jnp.int32)
    first_flag = (column_index == 0)[None, None, :]
    scores = raw_scores * LENGTH + column_index[None, None, :]
    scores = jnp.where(first_flag, -1, scores)
    ordered = jnp.sort(scores, axis=2)
    third_best = ordered[:, :, LENGTH - 3]
    starts = (scores >= third_best[:, :, None]) | first_flag
    row_number = jnp.arange(SEQS, dtype=jnp.int32)[None, :, None]
    starts = jnp.where(row_number == SEQS - 1, first_flag, starts)
    doc_numbers = jnp.cumsum(starts.astype(jnp.int32), axis=2) - 1
    doc_start = lax.cummax(jnp.where(starts, column_index[None, None, :], 0), axis=2)
    return (doc_numbers.astype(jnp.int32), (column_index[None, None, :] - doc_start).astype(jnp.int32))


def draw_doc_ids(key, part):
    return doc_layout(key)[0]


def draw_positions(key, part):
    return doc_layout(key)[1]


def draw_qkv_weight(key, part):
    draw_key = jax.random.fold_in(key, 13)
    columns = (HEADS + 2) * HEAD_DIM
    return (jnp.clip(jax.random.normal(draw_key, (D, columns), jnp.float32), -4.0, 4.0) / math.sqrt(D)).astype(jnp.bfloat16)


def draw_scale_query(key, part):
    draw_key = jax.random.fold_in(key, 11)
    return jax.random.uniform(draw_key, (HEAD_DIM,), jnp.float32, 0.5, 1.5)


def draw_scale_key(key, part):
    draw_key = jax.random.fold_in(key, 12)
    return jax.random.uniform(draw_key, (HEAD_DIM,), jnp.float32, 0.5, 1.5)


def raised(result, own_key, source, target, blocks, factor):
    owner, partner = [(jnp.arange(result.shape[dim]) // (result.shape[dim] // blocks)).reshape([-1 if axis == dim else 1 for axis in range(result.ndim)]) for dim in (source, target)]
    chosen = jax.random.permutation(own_key, blocks)[partner]
    strong = (owner == chosen) | (owner == (partner + blocks // 2) % blocks)
    return jnp.where(strong, factor * result, result)


def shard_levels(rng, extent, split, smallest, high):
    def one(position, blocks):
        heights = jax.random.uniform(jax.random.fold_in(jax.random.fold_in(rng, 6), position), (blocks,), jnp.float32, smallest / len(split), high / len(split))
        return jnp.repeat(jnp.exp(heights), extent[position] // blocks).reshape((-1,) + (1,) * (len(extent) - position - 1))

    level = one(*split[0])
    for cut in split[1:]:
        level = level * one(*cut)
    return level


def noise(stream_key, extent, width, bound, split=(), held_as=jnp.bfloat16):
    entries = jax.random.normal(stream_key, extent, jnp.float32) * width
    if len(split) > 0:
        entries = shard_levels(stream_key, extent, split, -0.22, 0.18) * entries
    return jnp.clip(entries, min=-bound, max=bound).astype(held_as)


def bell_draw_with(stream_key, shape, deviation, bound, shards, heavy, kind=jnp.bfloat16):
    entries = deviation * jax.random.normal(stream_key, shape, jnp.float32)
    if shards:
        entries = entries * shard_levels(stream_key, shape, shards, -0.22, 0.18)
    return jnp.clip(raised(entries, jax.random.fold_in(stream_key, 3), *heavy), -bound, bound).astype(kind)


def setup_inputs(seed: int = 0) -> dict:
    keys = jax.random.split(jax.random.key(seed), 15)
    return {
        "block_input": bell_draw_with(keys[0], (GROUPS, SEQS, LENGTH, D), 1.0, 6.0, ((0, 8), (2, 16)), (2, 3, 16, 2.0)),
        "doc_ids": draw_doc_ids(jax.random.fold_in(keys[14], 71), 0),
        "positions": draw_positions(jax.random.fold_in(keys[14], 71), 0),
        "qkv_weight": draw_qkv_weight(jax.random.fold_in(keys[14], 71), 0),
        "out_weight": noise(keys[4], (HEADS * HEAD_DIM, D), (HEADS * HEAD_DIM) ** -0.5, 0.1875, ((0, 8),)),
        "gate_up_weight": noise(keys[5], (D, 2 * FF), D ** -0.5, 0.1875, ((0, 8),)),
        "down_weight": noise(keys[6], (FF, D), FF ** -0.5, 0.078125, ((0, 8),)),
        "scale_attn_in": jnp.clip(1.0 + 0.18 * jax.random.normal(keys[7], (D,), jnp.float32), 0.1, 1.9),
        "scale_attn_out": jnp.clip(1.0 + 0.18 * jax.random.normal(keys[8], (D,), jnp.float32), 0.1, 1.9),
        "scale_ff_in": jnp.clip(1.0 + 0.18 * jax.random.normal(keys[9], (D,), jnp.float32), 0.1, 1.9),
        "scale_ff_out": jnp.clip(1.0 + 0.18 * jax.random.normal(keys[10], (D,), jnp.float32), 0.1, 1.9),
        "scale_query": draw_scale_query(jax.random.fold_in(keys[14], 71), 0),
        "scale_key": draw_scale_key(jax.random.fold_in(keys[14], 71), 0),
        "grad_output": noise(keys[13], (GROUPS, SEQS, LENGTH, D), 1.0, 6.0, ((0, 8), (2, 16))),
    }


NORM_EPS = 1e-06
ROPE_BASE = 1000000.0
GELU_COEF = 0.7978845608028654
GELU_CUBIC = 0.044715
MASK_FLOOR = -1e+30

def to_low(tensor):
    return lax.optimization_barrier(tensor.astype(jnp.bfloat16))

def rms_scale(tensor):
    return lax.rsqrt(lax.optimization_barrier(jnp.mean(tensor * tensor, axis=-1, keepdims=True)) + NORM_EPS)

def norm_back(tensor, scaled, gain_vector, cotangent):
    weighted = cotangent * gain_vector
    inner_mean = lax.optimization_barrier(jnp.mean(weighted * tensor, axis=-1, keepdims=True))
    return scaled * (weighted - tensor * scaled * scaled * inner_mean)

def rope_tables(positions):
    half_width = HEAD_DIM // 2
    frequency = ROPE_BASE ** (-2.0 * jnp.arange(half_width, dtype=jnp.float32) / HEAD_DIM)
    angles = positions.astype(jnp.float32)[..., None] * frequency
    return (jnp.cos(angles), jnp.sin(angles))

def rotate(tensor, cosine, sine_part):
    half_width = tensor.shape[-1] // 2
    leading = tensor[..., :half_width]
    trailing = tensor[..., half_width:]
    return jnp.concatenate([leading * cosine - trailing * sine_part, trailing * cosine + leading * sine_part], axis=-1)

def rotate_back(cotangent, cosine, sine_part):
    half_width = cotangent.shape[-1] // 2
    leading = cotangent[..., :half_width]
    trailing = cotangent[..., half_width:]
    return jnp.concatenate([leading * cosine + trailing * sine_part, trailing * cosine - leading * sine_part], axis=-1)

def gelu_parts(gate_part):
    tanh_input = GELU_COEF * (gate_part + GELU_CUBIC * gate_part * gate_part * gate_part)
    tanh_value = jnp.tanh(tanh_input)
    gelu_value = 0.5 * gate_part * (1.0 + tanh_value)
    gelu_slope = 0.5 * (1.0 + tanh_value) + 0.5 * gate_part * (1.0 - tanh_value * tanh_value) * GELU_COEF * (1.0 + 3.0 * GELU_CUBIC * gate_part * gate_part)
    return (gelu_value, gelu_slope)

def allowed_mask(query_pos, query_doc, key_pos, key_doc):
    same_doc = query_doc[:, :, None, None] == key_doc[:, None, None, :]
    causal = key_pos[:, None, None, :] <= query_pos[:, :, None, None]
    return same_doc & causal

def transposed_product(left_rows, right_rows):
    return lax.dot_general(left_rows, right_rows, (((1,), (1,)), ((), ())), preferred_element_type=jnp.float32)

def transposed_left(left_rows, right_rows):
    return lax.dot_general(left_rows, right_rows, (((0,), (0,)), ((), ())), preferred_element_type=jnp.float32)

def attention_forward(queries, key_rows, value_rows, allowed, score_scale):
    scores = jnp.einsum('bshd,bnd->bshn', queries.astype(jnp.float32), key_rows.astype(jnp.float32)) * score_scale
    masked = jnp.where(allowed, scores, MASK_FLOOR)
    best_score = lax.optimization_barrier(jnp.max(masked, axis=-1))
    weights = jnp.where(allowed, jnp.exp(scores - best_score[..., None]), 0.0)
    totals = lax.optimization_barrier(jnp.sum(weights, axis=-1))
    attended = jnp.einsum('bshn,bnd->bshd', weights, value_rows.astype(jnp.float32), precision=lax.Precision.HIGHEST) / totals[..., None]
    return (attended, best_score + jnp.log(totals))

def attention_backward(queries, key_rows, value_rows, allowed, score_scale, log_total, attended, attended_cot):
    scores = jnp.einsum('bshd,bnd->bshn', queries.astype(jnp.float32), key_rows.astype(jnp.float32)) * score_scale
    probabilities = jnp.where(allowed, jnp.exp(scores - log_total[..., None]), 0.0)
    cot_wide = attended_cot.astype(jnp.float32)
    row_delta = lax.optimization_barrier(jnp.sum(cot_wide * attended, axis=-1))
    prob_cot = jnp.einsum('bshd,bnd->bshn', cot_wide, value_rows.astype(jnp.float32))
    score_cot = to_low(probabilities * (prob_cot - row_delta[..., None])).astype(jnp.float32)
    query_cot = jnp.einsum('bshn,bnd->bshd', score_cot, key_rows.astype(jnp.float32)) * score_scale
    key_cot = jnp.einsum('bshn,bshd->bnd', score_cot, queries.astype(jnp.float32)) * score_scale
    prob_low = to_low(probabilities).astype(jnp.float32)
    value_cot = jnp.einsum('bshn,bshd->bnd', prob_low, cot_wide)
    return (query_cot, key_cot, value_cot)

def reference(block_input, doc_ids, positions, qkv_weight, out_weight, gate_up_weight, down_weight, scale_attn_in, scale_attn_out, scale_ff_in, scale_ff_out, scale_query, scale_key, grad_output):
    head_total = HEADS * HEAD_DIM
    score_scale = HEAD_DIM ** (-0.5)

    def one_group(running, inputs):
        group_input, group_doc, group_pos, group_cot = inputs
        seq_count = group_input.shape[0]
        seq_rows = group_input.shape[1]
        row_count = seq_count * seq_rows
        resid_in = group_input.reshape(row_count, D).astype(jnp.float32)
        scale_one = rms_scale(resid_in)
        attn_input = to_low(resid_in * scale_one * scale_attn_in)
        projected_qkv = jnp.dot(attn_input, qkv_weight, preferred_element_type=jnp.float32)
        query_raw = projected_qkv[:, :head_total].reshape(row_count, HEADS, HEAD_DIM)
        key_raw = projected_qkv[:, head_total:head_total + HEAD_DIM]
        value_rows = to_low(projected_qkv[:, head_total + HEAD_DIM:])
        query_scale = rms_scale(query_raw)
        key_scale = rms_scale(key_raw)
        cosine, sine_part = rope_tables(group_pos.reshape(row_count))
        queries = to_low(rotate(query_raw * query_scale * scale_query, cosine[:, None, :], sine_part[:, None, :]))
        key_rows = to_low(rotate(key_raw * key_scale * scale_key, cosine, sine_part))
        allowed = allowed_mask(group_pos, group_doc, group_pos, group_doc)
        query_blocks = queries.reshape(seq_count, seq_rows, HEADS, HEAD_DIM)
        key_blocks = key_rows.reshape(seq_count, seq_rows, HEAD_DIM)
        value_blocks = value_rows.reshape(seq_count, seq_rows, HEAD_DIM)
        attended, log_total = attention_forward(query_blocks, key_blocks, value_blocks, allowed, score_scale)
        attended_low = to_low(attended.reshape(row_count, head_total))
        projected = jnp.dot(attended_low, out_weight, preferred_element_type=jnp.float32)
        scale_two = rms_scale(projected)
        middle = resid_in + projected * scale_two * scale_attn_out
        scale_three = rms_scale(middle)
        ff_input = to_low(middle * scale_three * scale_ff_in)
        gate_up = jnp.dot(ff_input, gate_up_weight, preferred_element_type=jnp.float32)
        gate_part = gate_up[:, :FF]
        up_part = gate_up[:, FF:]
        gelu_value, gelu_slope = gelu_parts(gate_part)
        activation = to_low(gelu_value * up_part)
        down_out = jnp.dot(activation, down_weight, preferred_element_type=jnp.float32)
        scale_four = rms_scale(down_out)
        block_output = (middle + down_out * scale_four * scale_ff_out).astype(jnp.bfloat16)
        cotangent = group_cot.reshape(row_count, D).astype(jnp.float32)
        ff_out_part = lax.optimization_barrier(jnp.sum(cotangent * down_out * scale_four, axis=0))
        down_cot = to_low(norm_back(down_out, scale_four, scale_ff_out, cotangent))
        down_part = transposed_left(activation, down_cot)
        act_cot = transposed_product(down_cot, down_weight)
        gate_up_cot = to_low(jnp.concatenate([act_cot * up_part * gelu_slope, act_cot * gelu_value], axis=1))
        gate_up_part = transposed_left(ff_input, gate_up_cot)
        ff_input_cot = transposed_product(gate_up_cot, gate_up_weight)
        ff_in_part = lax.optimization_barrier(jnp.sum(ff_input_cot * middle * scale_three, axis=0))
        middle_cot = cotangent + norm_back(middle, scale_three, scale_ff_in, ff_input_cot)
        attn_out_part = lax.optimization_barrier(jnp.sum(middle_cot * projected * scale_two, axis=0))
        projected_cot = to_low(norm_back(projected, scale_two, scale_attn_out, middle_cot))
        out_part = transposed_left(attended_low, projected_cot)
        attended_cot = to_low(transposed_product(projected_cot, out_weight))
        query_cot, key_cot, value_cot = attention_backward(query_blocks, key_blocks, value_blocks, allowed, score_scale, log_total, attended, attended_cot.reshape(seq_count, seq_rows, HEADS, HEAD_DIM))
        query_back = rotate_back(query_cot.reshape(row_count, HEADS, HEAD_DIM), cosine[:, None, :], sine_part[:, None, :])
        key_back = rotate_back(key_cot.reshape(row_count, HEAD_DIM), cosine, sine_part)
        query_gain_part = lax.optimization_barrier(jnp.sum(query_back * query_raw * query_scale, axis=(0, 1)))
        key_gain_part = lax.optimization_barrier(jnp.sum(key_back * key_raw * key_scale, axis=0))
        qkv_cot = to_low(jnp.concatenate([norm_back(query_raw, query_scale, scale_query, query_back).reshape(row_count, head_total), norm_back(key_raw, key_scale, scale_key, key_back), value_cot.reshape(row_count, HEAD_DIM)], axis=1))
        qkv_part = transposed_left(attn_input, qkv_cot)
        attn_input_cot = transposed_product(qkv_cot, qkv_weight)
        attn_in_part = lax.optimization_barrier(jnp.sum(attn_input_cot * resid_in * scale_one, axis=0))
        input_grad = middle_cot + norm_back(resid_in, scale_one, scale_attn_in, attn_input_cot)
        parts = (qkv_part, out_part, gate_up_part, down_part, attn_in_part, attn_out_part, ff_in_part, ff_out_part, query_gain_part, key_gain_part)
        updated = tuple((total_now + part_now for total_now, part_now in zip(running, parts)))
        return (updated, (block_output.reshape(seq_count, seq_rows, D), input_grad.reshape(seq_count, seq_rows, D)))
    initial = (jnp.zeros((D, (HEADS + 2) * HEAD_DIM), jnp.float32), jnp.zeros((head_total, D), jnp.float32), jnp.zeros((D, 2 * FF), jnp.float32), jnp.zeros((FF, D), jnp.float32), jnp.zeros((D,), jnp.float32), jnp.zeros((D,), jnp.float32), jnp.zeros((D,), jnp.float32), jnp.zeros((D,), jnp.float32), jnp.zeros((HEAD_DIM,), jnp.float32), jnp.zeros((HEAD_DIM,), jnp.float32))
    totals, stacked = lax.scan(one_group, initial, (block_input, doc_ids, positions, grad_output))
    block_output, input_grad = stacked
    return (block_output, input_grad, totals[0], totals[1], totals[2], totals[3], totals[4], totals[5], totals[6], totals[7], totals[8], totals[9])
```

```python
import jax
import jax.numpy as jnp
from jax import lax
from jax.sharding import PartitionSpec as P

D = 1152
FF = 6912
HEADS = 4
HEAD_DIM = 256


NORM_EPS = 1e-06
ROPE_BASE = 1000000.0
GELU_COEF = 0.7978845608028654
GELU_CUBIC = 0.044715
MASK_FLOOR = -1e30


def rms_scale(tensor):
    return lax.rsqrt(jnp.mean(tensor * tensor, axis=-1, keepdims=True) + NORM_EPS)


def norm_back(tensor, scaled, gain_vector, cotangent):
    weighted = cotangent * gain_vector
    inner_mean = jnp.mean(weighted * tensor, axis=-1, keepdims=True)
    return scaled * (weighted - tensor * scaled * scaled * inner_mean)


def rope_tables(positions):
    half_width = HEAD_DIM // 2
    frequency = ROPE_BASE ** (-2.0 * jnp.arange(half_width, dtype=jnp.float32) / HEAD_DIM)
    angles = positions.astype(jnp.float32)[..., None] * frequency
    return (jnp.cos(angles), jnp.sin(angles))


def rotate(tensor, cosine, sine_part):
    half_width = tensor.shape[-1] // 2
    leading = tensor[..., :half_width]
    trailing = tensor[..., half_width:]
    return jnp.concatenate(
        [leading * cosine - trailing * sine_part, trailing * cosine + leading * sine_part], axis=-1
    )


def rotate_back(cotangent, cosine, sine_part):
    half_width = cotangent.shape[-1] // 2
    leading = cotangent[..., :half_width]
    trailing = cotangent[..., half_width:]
    return jnp.concatenate(
        [leading * cosine + trailing * sine_part, trailing * cosine - leading * sine_part], axis=-1
    )


def gelu_parts(gate_part):
    tanh_input = GELU_COEF * (gate_part + GELU_CUBIC * gate_part * gate_part * gate_part)
    tanh_value = jnp.tanh(tanh_input)
    gelu_value = 0.5 * gate_part * (1.0 + tanh_value)
    gelu_slope = 0.5 * (1.0 + tanh_value) + 0.5 * gate_part * (
        1.0 - tanh_value * tanh_value
    ) * GELU_COEF * (1.0 + 3.0 * GELU_CUBIC * gate_part * gate_part)
    return (gelu_value, gelu_slope)


def allowed_mask(query_pos, query_index, key_count):
    key_index = jnp.arange(key_count, dtype=jnp.int32)[None, None, None, :]
    first = (query_index[None, :] - query_pos)[:, :, None, None]
    return (key_index >= first) & (key_index <= query_index[None, :, None, None])


def transposed_product(right_rows, pieces):
    return lax.dot_general(
        right_rows, pieces, (((1,), (1,)), ((), ())), preferred_element_type=jnp.float32
    )


def transposed_left(left_rows, right_rows):
    return lax.dot_general(
        left_rows, right_rows, (((0,), (0,)), ((), ())), preferred_element_type=jnp.float32
    )


def add_product(left_rows, pieces):
    return jnp.dot(left_rows, pieces, preferred_element_type=jnp.float32)


def ctx_gather(rows):
    return lax.all_gather(rows, "ctx", axis=0, tiled=True)


def swap_blocks(blocks, axis_name):
    return lax.all_to_all(blocks, axis_name, split_axis=0, concat_axis=0, tiled=True)


def scatter_sum(partial, axis_name):
    members = lax.axis_size(axis_name)
    blocks = partial.astype(jnp.bfloat16).reshape(members, -1, partial.shape[-1])
    return jnp.sum(swap_blocks(blocks, axis_name).astype(jnp.float32), axis=0)


def attention_forward(queries, key_rows, value_rows, allowed, score_scale):
    scores = (
        jnp.einsum("bshd,bnd->bshn", queries, key_rows, preferred_element_type=jnp.float32)
        * score_scale
    )
    masked = jnp.where(allowed, scores, MASK_FLOOR)
    best_score = jnp.max(masked, axis=-1)
    weights = jnp.where(allowed, jnp.exp(scores - best_score[..., None]), 0.0)
    totals = jnp.sum(weights, axis=-1)
    attended = (
        jnp.einsum(
            "bshn,bnd->bshd",
            weights,
            value_rows.astype(jnp.float32),
            precision=lax.Precision.HIGHEST,
        )
        / totals[..., None]
    )
    return (attended, best_score + jnp.log(totals))


def attention_backward(
    queries, key_rows, value_rows, allowed, score_scale, log_total, attended, attended_cot
):
    scores = (
        jnp.einsum("bshd,bnd->bshn", queries, key_rows, preferred_element_type=jnp.float32)
        * score_scale
    )
    probabilities = jnp.where(allowed, jnp.exp(scores - log_total[..., None]), 0.0)
    row_delta = jnp.sum(attended_cot.astype(jnp.float32) * attended, axis=-1)
    prob_cot = jnp.einsum(
        "bshd,bnd->bshn", attended_cot, value_rows, preferred_element_type=jnp.float32
    )
    score_cot = (probabilities * (prob_cot - row_delta[..., None])).astype(jnp.bfloat16)
    query_cot = (
        jnp.einsum("bshn,bnd->bshd", score_cot, key_rows, preferred_element_type=jnp.float32)
        * score_scale
    )
    key_cot = (
        jnp.einsum("bshn,bshd->bnd", score_cot, queries, preferred_element_type=jnp.float32)
        * score_scale
    )
    value_cot = jnp.einsum(
        "bshn,bshd->bnd",
        probabilities.astype(jnp.bfloat16),
        attended_cot,
        preferred_element_type=jnp.float32,
    )
    return (query_cot, key_cot, value_cot)


def on_device(
    block_input,
    doc_ids,
    positions,
    qkv_weight,
    out_weight,
    gate_up_weight,
    down_weight,
    scale_attn_in,
    scale_attn_out,
    scale_ff_in,
    scale_ff_out,
    scale_query,
    scale_key,
    grad_output,
):
    ctx_size = lax.axis_size("ctx")
    fsdp_size = lax.axis_size("fsdp")
    ctx_index = lax.axis_index("ctx")
    seq_count = block_input.shape[1]
    seq_rows = block_input.shape[2]
    row_count = seq_count * seq_rows
    key_count = ctx_size * seq_rows
    head_total = HEADS * HEAD_DIM
    score_scale = HEAD_DIM ** (-0.5)
    part = FF // ctx_size
    piece = part // fsdp_size
    qkv_rows = qkv_weight.shape[0] // ctx_size
    out_rows = out_weight.shape[0] // ctx_size
    qkv_full = lax.all_gather(
        lax.dynamic_slice_in_dim(qkv_weight, ctx_index * qkv_rows, qkv_rows, 0),
        ("fsdp", "ctx"),
        axis=0,
        tiled=True,
    )
    out_full = lax.all_gather(
        lax.dynamic_slice_in_dim(out_weight, ctx_index * out_rows, out_rows, 0),
        ("fsdp", "ctx"),
        axis=0,
        tiled=True,
    )
    down_piece = lax.ppermute(
        lax.dynamic_slice_in_dim(down_weight, ctx_index * piece, piece, 0),
        ("ctx", "fsdp"),
        [
            (c * fsdp_size + f, (c + ctx_size * f))
            for c in range(ctx_size)
            for f in range(fsdp_size)
        ],
    )
    down_part = lax.all_gather(down_piece, "fsdp", axis=0, tiled=True)
    gate_part_w = lax.all_gather(
        lax.dynamic_slice_in_dim(gate_up_weight, ctx_index * part, part, 1),
        "fsdp",
        axis=0,
        tiled=True,
    )
    up_part_w = lax.all_gather(
        lax.dynamic_slice_in_dim(gate_up_weight, FF + ctx_index * part, part, 1),
        "fsdp",
        axis=0,
        tiled=True,
    )
    resid_in = block_input.reshape(row_count, D).astype(jnp.float32)
    scale_one = rms_scale(resid_in)
    attn_input = (resid_in * scale_one * scale_attn_in).astype(jnp.bfloat16)
    projected_qkv = jnp.dot(attn_input, qkv_full, preferred_element_type=jnp.float32)
    query_raw = projected_qkv[:, :head_total].reshape(row_count, HEADS, HEAD_DIM)
    key_raw = projected_qkv[:, head_total : head_total + HEAD_DIM]
    value_rows = projected_qkv[:, head_total + HEAD_DIM :].astype(jnp.bfloat16)
    query_scale = rms_scale(query_raw)
    key_scale = rms_scale(key_raw)
    local_pos = positions.reshape(seq_count, seq_rows)
    cosine, sine_part = rope_tables(local_pos.reshape(row_count))
    queries = rotate(
        query_raw * query_scale * scale_query, cosine[:, None, :], sine_part[:, None, :]
    ).astype(jnp.bfloat16)
    key_rows = rotate(key_raw * key_scale * scale_key, cosine, sine_part).astype(jnp.bfloat16)
    key_value = ctx_gather(jnp.concatenate([key_rows, value_rows], axis=1))
    key_value = key_value.reshape(ctx_size, seq_count, seq_rows, 2 * HEAD_DIM)
    key_value = key_value.transpose(1, 0, 2, 3).reshape(seq_count, key_count, 2 * HEAD_DIM)
    key_all = key_value[:, :, :HEAD_DIM]
    value_all = key_value[:, :, HEAD_DIM:]
    query_index = ctx_index * seq_rows + jnp.arange(seq_rows, dtype=jnp.int32)
    allowed = allowed_mask(local_pos, query_index, key_count)
    query_blocks = queries.reshape(seq_count, seq_rows, HEADS, HEAD_DIM)
    attended, log_total = attention_forward(query_blocks, key_all, value_all, allowed, score_scale)
    attended_low = attended.reshape(row_count, head_total).astype(jnp.bfloat16)
    projected = jnp.dot(attended_low, out_full, preferred_element_type=jnp.float32)
    scale_two = rms_scale(projected)
    middle = resid_in + projected * scale_two * scale_attn_out
    scale_three = rms_scale(middle)
    ff_input = (middle * scale_three * scale_ff_in).astype(jnp.bfloat16)
    ff_all = ctx_gather(ff_input)
    gate_part = add_product(ff_all, gate_part_w)
    up_part = add_product(ff_all, up_part_w)
    gelu_value, gelu_slope = gelu_parts(gate_part)
    activation = (gelu_value * up_part).astype(jnp.bfloat16)
    down_out = scatter_sum(add_product(activation, down_part), "ctx")
    scale_four = rms_scale(down_out)
    block_output = (middle + down_out * scale_four * scale_ff_out).astype(jnp.bfloat16)
    cotangent = grad_output.reshape(row_count, D).astype(jnp.float32)
    ff_out_grad = jnp.sum(cotangent * down_out * scale_four, axis=0)
    down_cot = norm_back(down_out, scale_four, scale_ff_out, cotangent).astype(jnp.bfloat16)
    down_cot_all = ctx_gather(down_cot)
    act_cot = transposed_product(down_cot_all, down_part)
    gate_cot = (act_cot * up_part * gelu_slope).astype(jnp.bfloat16)
    up_cot = (act_cot * gelu_value).astype(jnp.bfloat16)
    ff_input_cot = scatter_sum(
        transposed_product(gate_cot, gate_part_w) + transposed_product(up_cot, up_part_w), "ctx"
    )
    gate_up_sum = scatter_sum(
        jnp.concatenate(
            [transposed_left(gate_cot, ff_all), transposed_left(up_cot, ff_all)], axis=0
        ),
        "fsdp",
    )
    down_grad = scatter_sum(transposed_left(activation, down_cot_all), "fsdp")
    half = fsdp_size // 2
    gate_up_grad = lax.ppermute(
        gate_up_sum,
        ("ctx", "fsdp"),
        [
            (
                c * fsdp_size + f,
                half * c + f % half + (f // half) * (ctx_size * half),
            )
            for c in range(ctx_size)
            for f in range(fsdp_size)
        ],
    ).T
    ff_in_grad = jnp.sum(ff_input_cot * middle * scale_three, axis=0)
    middle_cot = cotangent + norm_back(middle, scale_three, scale_ff_in, ff_input_cot)
    attn_out_grad = jnp.sum(middle_cot * projected * scale_two, axis=0)
    projected_cot = norm_back(projected, scale_two, scale_attn_out, middle_cot).astype(jnp.bfloat16)
    attended_cot = transposed_product(projected_cot, out_full).astype(jnp.bfloat16)
    query_cot, key_cot, value_cot = attention_backward(
        query_blocks,
        key_all,
        value_all,
        allowed,
        score_scale,
        log_total,
        attended,
        attended_cot.reshape(seq_count, seq_rows, HEADS, HEAD_DIM),
    )
    kv_partial = jnp.concatenate([key_cot, value_cot], axis=2).reshape(
        seq_count, ctx_size, seq_rows, 2 * HEAD_DIM
    )
    kv_local = scatter_sum(kv_partial.transpose(1, 0, 2, 3), "ctx")
    key_cot_local = kv_local[:, :HEAD_DIM]
    value_cot_local = kv_local[:, HEAD_DIM:]
    query_back = rotate_back(
        query_cot.reshape(row_count, HEADS, HEAD_DIM), cosine[:, None, :], sine_part[:, None, :]
    )
    key_back = rotate_back(key_cot_local, cosine, sine_part)
    query_gain_grad = jnp.sum(query_back * query_raw * query_scale, axis=(0, 1))
    key_gain_grad = jnp.sum(key_back * key_raw * key_scale, axis=0)
    qkv_cot = jnp.concatenate(
        [
            norm_back(query_raw, query_scale, scale_query, query_back).reshape(
                row_count, head_total
            ),
            norm_back(key_raw, key_scale, scale_key, key_back),
            value_cot_local,
        ],
        axis=1,
    ).astype(jnp.bfloat16)
    attn_input_cot = transposed_product(qkv_cot, qkv_full)
    attn_in_grad = jnp.sum(attn_input_cot * resid_in * scale_one, axis=0)
    input_grad = middle_cot + norm_back(resid_in, scale_one, scale_attn_in, attn_input_cot)
    qkv_sum = scatter_sum(scatter_sum(transposed_left(qkv_cot, attn_input), "ctx"), "fsdp")
    out_grad = scatter_sum(
        scatter_sum(transposed_left(attended_low, projected_cot), "ctx"), "fsdp"
    )
    gains = jnp.concatenate(
        [attn_in_grad, attn_out_grad, ff_in_grad, ff_out_grad, query_gain_grad, key_gain_grad]
    )
    gains = jnp.sum(lax.all_gather(gains, "ctx"), axis=0)
    gains = jnp.sum(lax.all_gather(gains, "fsdp"), axis=0)
    return (
        block_output.reshape(1, seq_count, seq_rows, D),
        input_grad.reshape(1, seq_count, seq_rows, D),
        qkv_sum.T,
        out_grad,
        gate_up_grad,
        down_grad,
        gains[:D],
        gains[D : 2 * D],
        gains[2 * D : 3 * D],
        gains[3 * D : 4 * D],
        gains[4 * D : 4 * D + HEAD_DIM],
        gains[4 * D + HEAD_DIM :],
    )


def solution(mesh):
    return jax.shard_map(
        on_device,
        mesh=mesh,
        in_specs=(
            P("fsdp", None, "ctx", None),
            P("fsdp", None, "ctx"),
            P("fsdp", None, "ctx"),
            P("fsdp", None),
            P("fsdp", None),
            P("fsdp", None),
            P("fsdp", None),
            P(),
            P(),
            P(),
            P(),
            P(),
            P(),
            P("fsdp", None, "ctx", None),
        ),
        out_specs=(
            P("fsdp", None, "ctx", None),
            P("fsdp", None, "ctx", None),
            P(None, ("ctx", "fsdp")),
            P(("ctx", "fsdp"), None),
            P(None, ("ctx", "fsdp")),
            P(("ctx", "fsdp"), None),
            P(),
            P(),
            P(),
            P(),
            P(),
            P(),
        ),
        check_vma=False,
    )
```

```python
import functools

import jax
import jax.numpy as jnp
from jax import lax
from jax.experimental import pallas as pl
from jax.experimental.pallas import tpu as pltpu
from jax.sharding import PartitionSpec as P

MESH = pl.DeviceIdType.MESH

D = 1152
FF = 6912
HEADS = 4
HEAD_DIM = 256


NORM_EPS = 1e-06
ROPE_BASE = 1000000.0
GELU_COEF = 0.7978845608028654
GELU_CUBIC = 0.044715
MASK_FLOOR = -1e30


def rms_scale(tensor):
    return lax.rsqrt(jnp.mean(tensor * tensor, axis=-1, keepdims=True) + NORM_EPS)


def norm_back(tensor, scaled, gain_vector, cotangent):
    weighted = cotangent * gain_vector
    inner_mean = jnp.mean(weighted * tensor, axis=-1, keepdims=True)
    return scaled * (weighted - tensor * scaled * scaled * inner_mean)


def rope_tables(positions):
    half_width = HEAD_DIM // 2
    frequency = ROPE_BASE ** (-2.0 * jnp.arange(half_width, dtype=jnp.float32) / HEAD_DIM)
    angles = positions.astype(jnp.float32)[..., None] * frequency
    return (jnp.cos(angles), jnp.sin(angles))


def rotate(tensor, cosine, sine_part):
    half_width = tensor.shape[-1] // 2
    leading = tensor[..., :half_width]
    trailing = tensor[..., half_width:]
    return jnp.concatenate(
        [leading * cosine - trailing * sine_part, trailing * cosine + leading * sine_part], axis=-1
    )


def rotate_back(cotangent, cosine, sine_part):
    half_width = cotangent.shape[-1] // 2
    leading = cotangent[..., :half_width]
    trailing = cotangent[..., half_width:]
    return jnp.concatenate(
        [leading * cosine + trailing * sine_part, trailing * cosine - leading * sine_part], axis=-1
    )


def gelu_parts(gate_part):
    tanh_input = GELU_COEF * (gate_part + GELU_CUBIC * gate_part * gate_part * gate_part)
    tanh_value = jnp.tanh(tanh_input)
    gelu_value = 0.5 * gate_part * (1.0 + tanh_value)
    gelu_slope = 0.5 * (1.0 + tanh_value) + 0.5 * gate_part * (
        1.0 - tanh_value * tanh_value
    ) * GELU_COEF * (1.0 + 3.0 * GELU_CUBIC * gate_part * gate_part)
    return (gelu_value, gelu_slope)


def allowed_mask(query_pos, query_index, key_count):
    key_index = jnp.arange(key_count, dtype=jnp.int32)[None, None, None, :]
    first = (query_index[None, :] - query_pos)[:, :, None, None]
    return (key_index >= first) & (key_index <= query_index[None, :, None, None])


def transposed_product(right_rows, pieces):
    return lax.dot_general(
        right_rows, pieces, (((1,), (1,)), ((), ())), preferred_element_type=jnp.float32
    )


def transposed_left(left_rows, right_rows):
    return lax.dot_general(
        left_rows, right_rows, (((0,), (0,)), ((), ())), preferred_element_type=jnp.float32
    )


def add_product(left_rows, pieces):
    return jnp.dot(left_rows, pieces, preferred_element_type=jnp.float32)


def meet(axis_peers):
    barrier = pltpu.get_barrier_semaphore()
    for peer in axis_peers:
        pl.semaphore_signal(barrier, inc=1, device_id=peer, device_id_type=MESH)
    pl.semaphore_wait(barrier, len(axis_peers))


def remote(source, target, send_sem, recv_sem, peer):
    return pltpu.make_async_remote_copy(
        src_ref=source,
        dst_ref=target,
        send_sem=send_sem,
        recv_sem=recv_sem,
        device_id=peer,
        device_id_type=MESH,
    )


def gather_body(chips, x_ref, o_ref, send, recv, pass_send, pass_recv, own_sem):
    me = lax.axis_index("ctx")
    core = lax.rem(me, 2)
    chip = me // 2
    sibling = {"ctx": chip * 2 + 1 - core}
    slots = [(chip ^ r) * 2 + core for r in range(chips)]
    meet([sibling] + [{"ctx": slots[r]} for r in range(1, chips)])
    own = pltpu.make_async_copy(x_ref, o_ref.at[me], own_sem)
    own.start()
    copies = []
    for r in range(1, chips):
        copies.append(remote(x_ref, o_ref.at[me], send.at[r], recv.at[r], {"ctx": slots[r]}))
        copies[-1].start()
    passed = [remote(x_ref, o_ref.at[me], pass_send.at[0], pass_recv.at[0], sibling)]
    passed[0].start()
    for r in range(1, chips):
        copies[r - 1].wait_recv()
        block = o_ref.at[slots[r]]
        passed.append(remote(block, block, pass_send.at[r], pass_recv.at[r], sibling))
        passed[-1].start()
    own.wait()
    for copy in copies:
        copy.wait_send()
    for copy in passed:
        copy.wait()


def ctx_gather(rows, collective_id):
    members = lax.axis_size("ctx")
    chips = members // 2
    count, width = rows.shape
    gathered = pl.pallas_call(
        functools.partial(gather_body, chips),
        out_shape=jax.ShapeDtypeStruct((members, count, width), rows.dtype),
        in_specs=[pl.BlockSpec(memory_space=pltpu.VMEM)],
        out_specs=pl.BlockSpec(memory_space=pl.ANY),
        scratch_shapes=[pltpu.SemaphoreType.DMA((chips,))] * 4 + [pltpu.SemaphoreType.DMA],
        compiler_params=pltpu.CompilerParams(collective_id=collective_id, has_side_effects=True),
        name="ctx_gather",
    )(rows)
    return gathered.reshape(members * count, width)


def scatter_body(
    chips, rows, p_ref, o_ref, near, sums, far, near_send, near_recv, send, recv
):
    me = lax.axis_index("ctx")
    core = lax.rem(me, 2)
    chip = me // 2
    sibling = {"ctx": chip * 2 + 1 - core}
    slots = [(chip ^ r) * 2 + core for r in range(chips)]
    meet([sibling] + [{"ctx": slots[r]} for r in range(1, chips)])
    order = list(range(chips - 1, -1, -1))
    steps = p_ref.shape[1] // rows
    first = {}
    for r in order:
        block = p_ref.at[(chip ^ r) * 2 + 1 - core]
        first[r] = remote(block, near.at[r], near_send.at[r], near_recv.at[r], sibling)
        first[r].start()
    second = {}
    for r in order:
        first[r].wait_recv()
        if r:

            @pl.loop(0, steps)
            def _(i):
                part = pl.ds(pl.multiple_of(i * rows, rows), rows)
                total = p_ref[slots[r], part, :].astype(jnp.float32) + near[r, part, :].astype(
                    jnp.float32
                )
                sums[r, part, :] = total.astype(jnp.bfloat16)

            second[r] = remote(sums.at[r], far.at[r], send.at[r], recv.at[r], {"ctx": slots[r]})
        if r + 1 < chips:
            second[r + 1].start()
    for r in order[:-1]:
        second[r].wait_recv()

    @pl.loop(0, steps)
    def _(i):
        part = pl.ds(pl.multiple_of(i * rows, rows), rows)
        total = p_ref[slots[0], part, :].astype(jnp.float32) + near[0, part, :].astype(jnp.float32)
        for r in order[:-1]:
            total = total + far[r, part, :].astype(jnp.float32)
        o_ref[part, :] = total

    for r in order:
        first[r].wait_send()
    for r in order[:-1]:
        second[r].wait_send()


def ctx_scatter(partial, collective_id):
    members = lax.axis_size("ctx")
    chips = members // 2
    width = partial.shape[-1]
    blocks = partial.astype(jnp.bfloat16).reshape(members, -1, width)
    count = blocks.shape[1]
    buffer = pltpu.VMEM((chips, count, width), jnp.bfloat16)
    return pl.pallas_call(
        functools.partial(scatter_body, chips, 16),
        out_shape=jax.ShapeDtypeStruct((count, width), jnp.float32),
        in_specs=[pl.BlockSpec(memory_space=pltpu.VMEM)],
        out_specs=pl.BlockSpec(memory_space=pltpu.VMEM),
        scratch_shapes=[buffer] * 3 + [pltpu.SemaphoreType.DMA((chips,))] * 4,
        compiler_params=pltpu.CompilerParams(collective_id=collective_id, has_side_effects=True),
        name="ctx_scatter",
    )(blocks)


def weight_body(members, x_ref, o_ref, send, recv, pass_send, pass_recv, own_sem):
    ctx = lax.axis_index("ctx")
    core = lax.rem(ctx, 2)
    me = lax.axis_index("fsdp")
    sibling = {"ctx": (ctx // 2) * 2 + 1 - core}
    meet([sibling] + [{"fsdp": me ^ r} for r in range(1, members)])
    own = pltpu.make_async_copy(x_ref, o_ref.at[me], own_sem)
    own.start()
    copies = []
    for r in range(1, members):
        copies.append(
            remote(
                x_ref.at[core], o_ref.at[me, core], send.at[r], recv.at[r], {"fsdp": me ^ r}
            )
        )
        copies[-1].start()
    passed = []
    for r in range(1, members):
        copies[r - 1].wait_recv()
        block = o_ref.at[me ^ r, core]
        passed.append(remote(block, block, pass_send.at[r], pass_recv.at[r], sibling))
        passed[-1].start()
    own.wait()
    for copy in copies:
        copy.wait_send()
    for copy in passed:
        copy.wait()


def weight_gather(shard, collective_id):
    members = lax.axis_size("fsdp")
    rows, width = shard.shape
    halves = shard.reshape(2, rows // 2, width)
    gathered = pl.pallas_call(
        functools.partial(weight_body, members),
        out_shape=jax.ShapeDtypeStruct((members,) + halves.shape, shard.dtype),
        in_specs=[pl.BlockSpec(memory_space=pltpu.VMEM)],
        out_specs=pl.BlockSpec(memory_space=pl.ANY),
        scratch_shapes=[pltpu.SemaphoreType.DMA((members,))] * 4 + [pltpu.SemaphoreType.DMA],
        compiler_params=pltpu.CompilerParams(collective_id=collective_id, has_side_effects=True),
        name="weight_gather",
    )(halves)
    return gathered.reshape(members * rows, width)


def gain_body(ctx_size, fsdp_size, x_ref, o_ref, held, subtotal, others, send, recv, send2, recv2):
    ctx = lax.axis_index("ctx")
    fsdp = lax.axis_index("fsdp")
    ctx_peers = [{"ctx": ctx ^ r} for r in range(1, ctx_size)]
    fsdp_peers = [{"fsdp": fsdp ^ r} for r in range(1, fsdp_size)]
    meet(ctx_peers + fsdp_peers)
    held[ctx] = x_ref[...]
    copies = []
    for r in range(1, ctx_size):
        copies.append(remote(x_ref, held.at[ctx], send.at[r], recv.at[r], ctx_peers[r - 1]))
        copies[-1].start()
    for copy in copies:
        copy.wait()
    total = held[0]
    for i in range(1, ctx_size):
        total = total + held[i]
    subtotal[...] = total
    others[fsdp] = total
    copies = []
    for r in range(1, fsdp_size):
        copies.append(
            remote(subtotal, others.at[fsdp], send2.at[r], recv2.at[r], fsdp_peers[r - 1])
        )
        copies[-1].start()
    for copy in copies:
        copy.wait()
    total = others[0]
    for i in range(1, fsdp_size):
        total = total + others[i]
    o_ref[...] = total


def gain_sum(vector, collective_id):
    ctx_size = lax.axis_size("ctx")
    fsdp_size = lax.axis_size("fsdp")
    rows = vector.reshape(-1, 128)
    return pl.pallas_call(
        functools.partial(gain_body, ctx_size, fsdp_size),
        out_shape=jax.ShapeDtypeStruct(rows.shape, jnp.float32),
        in_specs=[pl.BlockSpec(memory_space=pltpu.VMEM)],
        out_specs=pl.BlockSpec(memory_space=pltpu.VMEM),
        scratch_shapes=[
            pltpu.VMEM((ctx_size,) + rows.shape, jnp.float32),
            pltpu.VMEM(rows.shape, jnp.float32),
            pltpu.VMEM((fsdp_size,) + rows.shape, jnp.float32),
        ]
        + [pltpu.SemaphoreType.DMA((ctx_size,))] * 2
        + [pltpu.SemaphoreType.DMA((fsdp_size,))] * 2,
        compiler_params=pltpu.CompilerParams(collective_id=collective_id, has_side_effects=True),
        name="gain_sum",
    )(rows).reshape(-1)


def spread(shard, axis_name):
    members = lax.axis_size(axis_name)
    copies = jnp.broadcast_to(shard[None], (members,) + shard.shape)
    return swap_blocks(copies, axis_name).reshape(members * shard.shape[0], shard.shape[1])


def swap_blocks(blocks, axis_name):
    return lax.all_to_all(blocks, axis_name, split_axis=0, concat_axis=0, tiled=True)


def scatter_sum(partial, axis_name):
    members = lax.axis_size(axis_name)
    blocks = partial.astype(jnp.bfloat16).reshape(members, -1, partial.shape[-1])
    return jnp.sum(swap_blocks(blocks, axis_name).astype(jnp.float32), axis=0)


def attention_forward(queries, key_rows, value_rows, allowed, score_scale):
    scores = (
        jnp.einsum("bshd,bnd->bshn", queries, key_rows, preferred_element_type=jnp.float32)
        * score_scale
    )
    masked = jnp.where(allowed, scores, MASK_FLOOR)
    best_score = jnp.max(masked, axis=-1)
    weights = jnp.where(allowed, jnp.exp(scores - best_score[..., None]), 0.0)
    totals = jnp.sum(weights, axis=-1)
    attended = (
        jnp.einsum(
            "bshn,bnd->bshd",
            weights,
            value_rows.astype(jnp.float32),
            precision=lax.Precision.HIGHEST,
        )
        / totals[..., None]
    )
    return (attended, best_score + jnp.log(totals))


def attention_backward(
    queries, key_rows, value_rows, allowed, score_scale, log_total, attended, attended_cot
):
    scores = (
        jnp.einsum("bshd,bnd->bshn", queries, key_rows, preferred_element_type=jnp.float32)
        * score_scale
    )
    probabilities = jnp.where(allowed, jnp.exp(scores - log_total[..., None]), 0.0)
    row_delta = jnp.sum(attended_cot.astype(jnp.float32) * attended, axis=-1)
    prob_cot = jnp.einsum(
        "bshd,bnd->bshn", attended_cot, value_rows, preferred_element_type=jnp.float32
    )
    score_cot = (probabilities * (prob_cot - row_delta[..., None])).astype(jnp.bfloat16)
    query_cot = (
        jnp.einsum("bshn,bnd->bshd", score_cot, key_rows, preferred_element_type=jnp.float32)
        * score_scale
    )
    key_cot = (
        jnp.einsum("bshn,bshd->bnd", score_cot, queries, preferred_element_type=jnp.float32)
        * score_scale
    )
    value_cot = jnp.einsum(
        "bshn,bshd->bnd",
        probabilities.astype(jnp.bfloat16),
        attended_cot,
        preferred_element_type=jnp.float32,
    )
    return (query_cot, key_cot, value_cot)


def on_device(
    block_input,
    doc_ids,
    positions,
    qkv_weight,
    out_weight,
    gate_up_weight,
    down_weight,
    scale_attn_in,
    scale_attn_out,
    scale_ff_in,
    scale_ff_out,
    scale_query,
    scale_key,
    grad_output,
):
    ctx_size = lax.axis_size("ctx")
    fsdp_size = lax.axis_size("fsdp")
    ctx_index = lax.axis_index("ctx")
    seq_count = block_input.shape[1]
    seq_rows = block_input.shape[2]
    row_count = seq_count * seq_rows
    key_count = ctx_size * seq_rows
    head_total = HEADS * HEAD_DIM
    score_scale = HEAD_DIM ** (-0.5)
    part = FF // ctx_size
    piece = part // fsdp_size
    qkv_full = weight_gather(qkv_weight, 1)
    out_full = weight_gather(out_weight, 2)
    down_piece = lax.ppermute(
        lax.dynamic_slice_in_dim(down_weight, ctx_index * piece, piece, 0),
        ("ctx", "fsdp"),
        [
            (c * fsdp_size + f, (c + ctx_size * f))
            for c in range(ctx_size)
            for f in range(fsdp_size)
        ],
    )
    down_part = spread(down_piece, "fsdp")
    gate_part_w = spread(
        lax.dynamic_slice_in_dim(gate_up_weight, ctx_index * part, part, 1), "fsdp"
    )
    up_part_w = spread(
        lax.dynamic_slice_in_dim(gate_up_weight, FF + ctx_index * part, part, 1), "fsdp"
    )
    resid_in = block_input.reshape(row_count, D).astype(jnp.float32)
    scale_one = rms_scale(resid_in)
    attn_input = (resid_in * scale_one * scale_attn_in).astype(jnp.bfloat16)
    projected_qkv = jnp.dot(attn_input, qkv_full, preferred_element_type=jnp.float32)
    query_raw = projected_qkv[:, :head_total].reshape(row_count, HEADS, HEAD_DIM)
    key_raw = projected_qkv[:, head_total : head_total + HEAD_DIM]
    value_rows = projected_qkv[:, head_total + HEAD_DIM :].astype(jnp.bfloat16)
    query_scale = rms_scale(query_raw)
    key_scale = rms_scale(key_raw)
    local_pos = positions.reshape(seq_count, seq_rows)
    cosine, sine_part = rope_tables(local_pos.reshape(row_count))
    queries = rotate(
        query_raw * query_scale * scale_query, cosine[:, None, :], sine_part[:, None, :]
    ).astype(jnp.bfloat16)
    key_rows = rotate(key_raw * key_scale * scale_key, cosine, sine_part).astype(jnp.bfloat16)
    key_value = ctx_gather(jnp.concatenate([key_rows, value_rows], axis=1), 3)
    key_value = key_value.reshape(ctx_size, seq_count, seq_rows, 2 * HEAD_DIM)
    key_value = key_value.transpose(1, 0, 2, 3).reshape(seq_count, key_count, 2 * HEAD_DIM)
    key_all = key_value[:, :, :HEAD_DIM]
    value_all = key_value[:, :, HEAD_DIM:]
    query_index = ctx_index * seq_rows + jnp.arange(seq_rows, dtype=jnp.int32)
    allowed = allowed_mask(local_pos, query_index, key_count)
    query_blocks = queries.reshape(seq_count, seq_rows, HEADS, HEAD_DIM)
    attended, log_total = attention_forward(query_blocks, key_all, value_all, allowed, score_scale)
    attended_low = attended.reshape(row_count, head_total).astype(jnp.bfloat16)
    projected = jnp.dot(attended_low, out_full, preferred_element_type=jnp.float32)
    scale_two = rms_scale(projected)
    middle = resid_in + projected * scale_two * scale_attn_out
    scale_three = rms_scale(middle)
    ff_input = (middle * scale_three * scale_ff_in).astype(jnp.bfloat16)
    ff_all = ctx_gather(ff_input, 4)
    gate_part = add_product(ff_all, gate_part_w)
    up_part = add_product(ff_all, up_part_w)
    gelu_value, gelu_slope = gelu_parts(gate_part)
    activation = (gelu_value * up_part).astype(jnp.bfloat16)
    down_out = ctx_scatter(add_product(activation, down_part), 6)
    scale_four = rms_scale(down_out)
    block_output = (middle + down_out * scale_four * scale_ff_out).astype(jnp.bfloat16)
    cotangent = grad_output.reshape(row_count, D).astype(jnp.float32)
    ff_out_grad = jnp.sum(cotangent * down_out * scale_four, axis=0)
    down_cot = norm_back(down_out, scale_four, scale_ff_out, cotangent).astype(jnp.bfloat16)
    down_cot_all = ctx_gather(down_cot, 5)
    act_cot = transposed_product(down_cot_all, down_part)
    gate_cot = (act_cot * up_part * gelu_slope).astype(jnp.bfloat16)
    up_cot = (act_cot * gelu_value).astype(jnp.bfloat16)
    ff_input_cot = ctx_scatter(
        transposed_product(gate_cot, gate_part_w) + transposed_product(up_cot, up_part_w), 7
    )
    gate_up_sum = scatter_sum(
        jnp.concatenate(
            [transposed_left(gate_cot, ff_all), transposed_left(up_cot, ff_all)], axis=0
        ),
        "fsdp",
    )
    down_grad = scatter_sum(transposed_left(activation, down_cot_all), "fsdp")
    half = fsdp_size // 2
    gate_up_grad = lax.ppermute(
        gate_up_sum,
        ("ctx", "fsdp"),
        [
            (
                c * fsdp_size + f,
                half * c + f % half + (f // half) * (ctx_size * half),
            )
            for c in range(ctx_size)
            for f in range(fsdp_size)
        ],
    ).T
    ff_in_grad = jnp.sum(ff_input_cot * middle * scale_three, axis=0)
    middle_cot = cotangent + norm_back(middle, scale_three, scale_ff_in, ff_input_cot)
    attn_out_grad = jnp.sum(middle_cot * projected * scale_two, axis=0)
    projected_cot = norm_back(projected, scale_two, scale_attn_out, middle_cot).astype(jnp.bfloat16)
    attended_cot = transposed_product(projected_cot, out_full).astype(jnp.bfloat16)
    query_cot, key_cot, value_cot = attention_backward(
        query_blocks,
        key_all,
        value_all,
        allowed,
        score_scale,
        log_total,
        attended,
        attended_cot.reshape(seq_count, seq_rows, HEADS, HEAD_DIM),
    )
    kv_partial = jnp.concatenate([key_cot, value_cot], axis=2).reshape(
        seq_count, ctx_size, seq_rows, 2 * HEAD_DIM
    )
    kv_local = ctx_scatter(kv_partial.transpose(1, 0, 2, 3), 8)
    key_cot_local = kv_local[:, :HEAD_DIM]
    value_cot_local = kv_local[:, HEAD_DIM:]
    query_back = rotate_back(
        query_cot.reshape(row_count, HEADS, HEAD_DIM), cosine[:, None, :], sine_part[:, None, :]
    )
    key_back = rotate_back(key_cot_local, cosine, sine_part)
    query_gain_grad = jnp.sum(query_back * query_raw * query_scale, axis=(0, 1))
    key_gain_grad = jnp.sum(key_back * key_raw * key_scale, axis=0)
    qkv_cot = jnp.concatenate(
        [
            norm_back(query_raw, query_scale, scale_query, query_back).reshape(
                row_count, head_total
            ),
            norm_back(key_raw, key_scale, scale_key, key_back),
            value_cot_local,
        ],
        axis=1,
    ).astype(jnp.bfloat16)
    attn_input_cot = transposed_product(qkv_cot, qkv_full)
    attn_in_grad = jnp.sum(attn_input_cot * resid_in * scale_one, axis=0)
    input_grad = middle_cot + norm_back(resid_in, scale_one, scale_attn_in, attn_input_cot)
    qkv_sum = scatter_sum(ctx_scatter(transposed_left(qkv_cot, attn_input), 9), "fsdp")
    out_grad = scatter_sum(
        ctx_scatter(transposed_left(attended_low, projected_cot), 10), "fsdp"
    )
    gains = jnp.concatenate(
        [attn_in_grad, attn_out_grad, ff_in_grad, ff_out_grad, query_gain_grad, key_gain_grad]
    )
    gains = gain_sum(gains, 11)
    return (
        block_output.reshape(1, seq_count, seq_rows, D),
        input_grad.reshape(1, seq_count, seq_rows, D),
        qkv_sum.T,
        out_grad,
        gate_up_grad,
        down_grad,
        gains[:D],
        gains[D : 2 * D],
        gains[2 * D : 3 * D],
        gains[3 * D : 4 * D],
        gains[4 * D : 4 * D + HEAD_DIM],
        gains[4 * D + HEAD_DIM :],
    )


def solution(mesh):
    return jax.shard_map(
        on_device,
        mesh=mesh,
        in_specs=(
            P("fsdp", None, "ctx", None),
            P("fsdp", None, "ctx"),
            P("fsdp", None, "ctx"),
            P("fsdp", None),
            P("fsdp", None),
            P("fsdp", None),
            P("fsdp", None),
            P(),
            P(),
            P(),
            P(),
            P(),
            P(),
            P("fsdp", None, "ctx", None),
        ),
        out_specs=(
            P("fsdp", None, "ctx", None),
            P("fsdp", None, "ctx", None),
            P(None, ("ctx", "fsdp")),
            P(("ctx", "fsdp"), None),
            P(None, ("ctx", "fsdp")),
            P(("ctx", "fsdp"), None),
            P(),
            P(),
            P(),
            P(),
            P(),
            P(),
        ),
        check_vma=False,
    )
```

```python
import functools

import jax
import jax.numpy as jnp
from jax import lax
from jax.experimental import pallas as pl
from jax.experimental.pallas import tpu as pltpu
from jax.sharding import PartitionSpec as P

MESH = pl.DeviceIdType.MESH

D = 1152
FF = 6912
HEADS = 4
HEAD_DIM = 256


NORM_EPS = 1e-06
ROPE_BASE = 1000000.0
GELU_COEF = 0.7978845608028654
GELU_CUBIC = 0.044715
MASK_FLOOR = -1e30


def rms_scale(tensor):
    return lax.rsqrt(jnp.mean(tensor * tensor, axis=-1, keepdims=True) + NORM_EPS)


def norm_back(tensor, scaled, gain_vector, cotangent):
    weighted = cotangent * gain_vector
    inner_mean = jnp.mean(weighted * tensor, axis=-1, keepdims=True)
    return scaled * (weighted - tensor * scaled * scaled * inner_mean)


def rope_tables(positions):
    half_width = HEAD_DIM // 2
    frequency = ROPE_BASE ** (-2.0 * jnp.arange(half_width, dtype=jnp.float32) / HEAD_DIM)
    angles = positions.astype(jnp.float32)[..., None] * frequency
    return (jnp.cos(angles), jnp.sin(angles))


def rotate(tensor, cosine, sine_part):
    half_width = tensor.shape[-1] // 2
    leading = tensor[..., :half_width]
    trailing = tensor[..., half_width:]
    return jnp.concatenate(
        [leading * cosine - trailing * sine_part, trailing * cosine + leading * sine_part], axis=-1
    )


def rotate_back(cotangent, cosine, sine_part):
    half_width = cotangent.shape[-1] // 2
    leading = cotangent[..., :half_width]
    trailing = cotangent[..., half_width:]
    return jnp.concatenate(
        [leading * cosine + trailing * sine_part, trailing * cosine - leading * sine_part], axis=-1
    )


def gelu_parts(gate_part):
    tanh_input = GELU_COEF * (gate_part + GELU_CUBIC * gate_part * gate_part * gate_part)
    tanh_value = jnp.tanh(tanh_input)
    gelu_value = 0.5 * gate_part * (1.0 + tanh_value)
    gelu_slope = 0.5 * (1.0 + tanh_value) + 0.5 * gate_part * (
        1.0 - tanh_value * tanh_value
    ) * GELU_COEF * (1.0 + 3.0 * GELU_CUBIC * gate_part * gate_part)
    return (gelu_value, gelu_slope)


def allowed_mask(query_pos, query_index, key_count):
    key_index = jnp.arange(key_count, dtype=jnp.int32)[None, None, None, :]
    first = (query_index[None, :] - query_pos)[:, :, None, None]
    return (key_index >= first) & (key_index <= query_index[None, :, None, None])


def transposed_product(right_rows, pieces):
    return lax.dot_general(
        right_rows, pieces, (((1,), (1,)), ((), ())), preferred_element_type=jnp.float32
    )


def transposed_left(left_rows, right_rows):
    return lax.dot_general(
        left_rows, right_rows, (((0,), (0,)), ((), ())), preferred_element_type=jnp.float32
    )


def add_product(left_rows, pieces):
    return jnp.dot(left_rows, pieces, preferred_element_type=jnp.float32)


def meet(axis_peers):
    barrier = pltpu.get_barrier_semaphore()
    for peer in axis_peers:
        pl.semaphore_signal(barrier, inc=1, device_id=peer, device_id_type=MESH)
    pl.semaphore_wait(barrier, len(axis_peers))


def remote(source, target, send_sem, recv_sem, peer):
    return pltpu.make_async_remote_copy(
        src_ref=source,
        dst_ref=target,
        send_sem=send_sem,
        recv_sem=recv_sem,
        device_id=peer,
        device_id_type=MESH,
    )


LABELS = ("me", "up", "down", "far", "cross", "xup", "xdown", "xfar")


def ctx_place():
    me = lax.axis_index("ctx")
    core = lax.rem(me, 2)
    ring = lax.rem(me // 2, 4)
    pair = me // 8
    sibling = {"ctx": me + 1 - 2 * core}
    rings = {"me": ring, "up": lax.rem(ring + 1, 4), "down": lax.rem(ring + 3, 4)}
    rings["far"] = lax.rem(ring + 2, 4)
    slots = {}
    for name, where in rings.items():
        slots[name] = pair * 8 + where * 2
        slots["cross" if name == "me" else "x" + name] = (1 - pair) * 8 + where * 2
    peers = {name: {"ctx": slots[name] + core} for name in ("up", "down", "cross")}
    return core, sibling, slots, peers


def fsdp_place():
    ctx = lax.axis_index("ctx")
    me = lax.axis_index("fsdp")
    core = lax.rem(ctx, 2)
    ring = me // 2
    pair = lax.rem(me, 2)
    sibling = {"ctx": ctx + 1 - 2 * core}
    rings = {"me": ring, "up": lax.rem(ring + 1, 4), "down": lax.rem(ring + 3, 4)}
    rings["far"] = lax.rem(ring + 2, 4)
    slots = {}
    for name, where in rings.items():
        slots[name] = where * 2 + pair
        slots["cross" if name == "me" else "x" + name] = where * 2 + 1 - pair
    peers = {name: {"fsdp": slots[name]} for name in ("up", "down")}
    peers["cross"] = {"ctx": lax.rem(ctx + 8, 16), "fsdp": slots["cross"]}
    return core, sibling, slots, peers


class Gather:
    def __init__(self, kind, x_ref, o_ref, sems):
        self.kind, self.o_ref = kind, o_ref
        self.core, self.sibling, self.slots, self.peers = (
            ctx_place() if kind == "ctx" else fsdp_place()
        )
        self.send, self.recv, self.pass_send, self.pass_recv, self.own_sem = sems
        self.x_ref = x_ref
        self.own = x_ref if kind == "ctx" else x_ref.at[self.core]
        rows = self.own.shape[0]
        first = (rows // 2 + 7) // 8 * 8
        self.halves = (pl.ds(0, first), pl.ds(first, rows - first))
        self.waits = []
        self.arrivals = {}

    def block(self, name, part=None):
        if self.kind == "ctx":
            index = (self.slots[name] + self.core,)
        else:
            index = (self.slots[name], self.core)
        return self.o_ref.at[index if part is None else index + (part,)]

    def forward(self, index, source, target, arrival, peer):
        copy = remote(source, target, self.send.at[index], self.recv.at[arrival], self.peers[peer])
        copy.start()
        self.waits.append(copy)
        return copy

    def arrived(self, arrival, name, part=None):
        block = self.block(name, part)
        remote(block, block, self.send.at[0], self.recv.at[arrival], self.peers["up"]).wait_recv()

    def hand_over(self, index, name, source=None):
        block = self.block(name)
        copy = remote(
            block if source is None else source,
            block,
            self.pass_send.at[index],
            self.pass_recv.at[index],
            self.sibling,
        )
        copy.start()
        self.arrivals[index] = copy

    def stage(self, number):
        if number == 0:
            if self.kind == "ctx":
                here = self.block("me")
            else:
                here = self.o_ref.at[self.slots["me"]]
            self.local = pltpu.make_async_copy(self.x_ref, here, self.own_sem)
            self.local.start()
            self.forward(0, self.own, self.block("me"), 1, "up")
            self.forward(1, self.own, self.block("me"), 0, "down")
            self.forward(2, self.own, self.block("me"), 2, "cross")
            if self.kind == "ctx":
                self.hand_over(0, "me", self.own)
        elif number == 1:
            self.arrived(1, "down")
            part = self.block("down", self.halves[0])
            self.forward(3, part, part, 3, "up")
            self.hand_over(1, "down")
            self.arrived(0, "up")
            part = self.block("up", self.halves[1])
            self.forward(4, part, part, 4, "down")
            self.hand_over(2, "up")
        elif number == 2:
            self.arrived(2, "cross")
            block = self.block("cross")
            self.forward(5, block, block, 5, "up")
            self.forward(6, block, block, 6, "down")
            self.hand_over(3, "cross")
        elif number == 3:
            self.arrived(3, "far", self.halves[0])
            self.arrived(4, "far", self.halves[1])
            block = self.block("far")
            self.forward(7, block, block, 7, "cross")
            self.hand_over(4, "far")
        elif number == 4:
            self.arrived(5, "xdown")
            self.hand_over(5, "xdown")
            self.arrived(6, "xup")
            self.hand_over(6, "xup")
        elif number == 5:
            self.arrived(7, "xfar")
            self.hand_over(7, "xfar")
        else:
            self.local.wait()
            for copy in self.waits:
                copy.wait_send()
            for copy in self.arrivals.values():
                copy.wait()


def gather_body(kinds, *refs):
    count = len(kinds)
    inputs, outputs, sems = refs[:count], refs[count : 2 * count], refs[2 * count :]
    jobs = [
        Gather(kind, inputs[i], outputs[i], sems[5 * i : 5 * i + 5])
        for i, kind in enumerate(kinds)
    ]
    greeted = [jobs[0].sibling]
    for i, job in enumerate(jobs):
        if job.kind not in kinds[:i]:
            greeted += [job.peers[name] for name in ("up", "down", "cross")]
    meet(greeted)
    for number in range(7):
        for job in jobs:
            job.stage(number)


def gather(kinds, arrays, collective_id):
    shaped, shapes = [], []
    for kind, array in zip(kinds, arrays):
        rows, width = array.shape
        if kind == "ctx":
            shaped.append(array)
            shapes.append((lax.axis_size("ctx"), rows, width))
        else:
            shaped.append(array.reshape(2, rows // 2, width))
            shapes.append((lax.axis_size("fsdp"), 2, rows // 2, width))
    gathered = pl.pallas_call(
        functools.partial(gather_body, kinds),
        out_shape=[jax.ShapeDtypeStruct(shape, jnp.bfloat16) for shape in shapes],
        in_specs=[pl.BlockSpec(memory_space=pltpu.VMEM)] * len(kinds),
        out_specs=[pl.BlockSpec(memory_space=pl.ANY)] * len(kinds),
        scratch_shapes=([pltpu.SemaphoreType.DMA((8,))] * 4 + [pltpu.SemaphoreType.DMA])
        * len(kinds),
        compiler_params=pltpu.CompilerParams(collective_id=collective_id, has_side_effects=True),
        name="gather_" + "_".join(kinds),
    )(*shaped)
    return [array.reshape(-1, array.shape[-1]) for array in gathered]


def scatter_body(
    rows, p_ref, o_ref, near, sums, held, near_send, near_recv, send, recv
):
    core, sibling, slots, peers = ctx_place()
    meet([sibling] + [peers[name] for name in ("up", "down", "cross")])
    count = p_ref.shape[1]
    half = count // 2
    halves = (pl.ds(0, half), pl.ds(half, half))
    order = ("xfar", "xup", "xdown", "up", "down", "far", "cross", "me")
    number = {name: i for i, name in enumerate(LABELS)}
    first = {}
    for name in order:
        i = number[name]
        first[name] = remote(
            p_ref.at[slots[name] + 1 - core],
            near.at[i],
            near_send.at[i],
            near_recv.at[i],
            sibling,
        )
        first[name].start()

    def add_up(name, target, start, stop, extras=()):
        i = number[name]

        @pl.loop(start // rows, stop // rows)
        def _(step):
            part = pl.ds(pl.multiple_of(step * rows, rows), rows)
            total = p_ref[slots[name] + core, part, :].astype(jnp.float32)
            total = total + near[i, part, :].astype(jnp.float32)
            for extra in extras:
                total = total + held[extra, part, :].astype(jnp.float32)
            if target is None:
                sums[i, part, :] = total.astype(jnp.bfloat16)
            else:
                target[part, :] = total

    started = []

    def push(index, name, slot, arrival, peer, part=None):
        i = number[name]
        source = sums.at[i] if part is None else sums.at[i, part]
        target = held.at[slot] if part is None else held.at[slot, part]
        copy = remote(source, target, send.at[index], recv.at[arrival], peers[peer])
        copy.start()
        started.append(copy)

    def arrived(arrival, slot, part=None):
        block = held.at[slot] if part is None else held.at[slot, part]
        remote(block, block, send.at[0], recv.at[arrival], peers["up"]).wait_recv()

    first["xfar"].wait_recv()
    add_up("xfar", None, 0, count)
    first["xup"].wait_recv()
    add_up("xup", None, 0, count)
    push(0, "xfar", 0, 0, "cross")
    first["xdown"].wait_recv()
    add_up("xdown", None, 0, count)
    push(1, "xup", 2, 2, "up")
    first["up"].wait_recv()
    add_up("up", None, half, count)
    push(2, "xdown", 1, 1, "down")
    first["down"].wait_recv()
    add_up("down", None, 0, half)
    push(3, "up", 5, 5, "up", halves[1])
    first["far"].wait_recv()
    push(4, "down", 4, 4, "down", halves[0])
    arrived(0, 0)
    add_up("far", None, 0, half, (0,))
    add_up("far", None, half, count, (0,))
    push(5, "far", 3, 3, "up", halves[0])
    push(6, "far", 3, 8, "down", halves[1])
    first["cross"].wait_recv()
    arrived(1, 1)
    arrived(2, 2)
    add_up("cross", None, 0, count, (1, 2))
    arrived(3, 3, halves[0])
    add_up("up", None, 0, half, (3,))
    push(7, "cross", 6, 6, "cross")
    arrived(8, 3, halves[1])
    add_up("down", None, half, count, (3,))
    push(8, "up", 5, 7, "up", halves[0])
    first["me"].wait_recv()
    push(9, "down", 4, 9, "down", halves[1])
    arrived(6, 6)
    arrived(5, 5, halves[1])
    arrived(4, 4, halves[0])
    arrived(7, 5, halves[0])
    arrived(9, 4, halves[1])
    add_up("me", o_ref, 0, count, (4, 5, 6))
    for name in order:
        first[name].wait_send()
    for copy in started:
        copy.wait_send()


def ctx_scatter(partial, collective_id):
    members = lax.axis_size("ctx")
    width = partial.shape[-1]
    blocks = partial.astype(jnp.bfloat16).reshape(members, -1, width)
    count = blocks.shape[1]

    def buffer(number):
        return pltpu.VMEM((number, count, width), jnp.bfloat16)

    return pl.pallas_call(
        functools.partial(scatter_body, 16),
        out_shape=jax.ShapeDtypeStruct((count, width), jnp.float32),
        in_specs=[pl.BlockSpec(memory_space=pltpu.VMEM)],
        out_specs=pl.BlockSpec(memory_space=pltpu.VMEM),
        scratch_shapes=[buffer(8), buffer(8), buffer(7)]
        + [pltpu.SemaphoreType.DMA((8,))] * 2
        + [pltpu.SemaphoreType.DMA((10,))] * 2,
        compiler_params=pltpu.CompilerParams(collective_id=collective_id, has_side_effects=True),
        name="ctx_scatter",
    )(blocks)


def final_body(
    ctx_size, fsdp_size, x_ref, w_ref, o_ref, g_ref, held, subtotal, others, blocks, *sems
):
    send, recv, send2, recv2, send3, recv3 = sems
    ctx = lax.axis_index("ctx")
    fsdp = lax.axis_index("fsdp")
    ctx_peers = [{"ctx": ctx ^ r} for r in range(1, ctx_size)]
    fsdp_peers = [{"fsdp": fsdp ^ r} for r in range(1, fsdp_size)]
    meet(ctx_peers + fsdp_peers)
    held[ctx] = x_ref[...]
    copies = []
    for r in range(1, ctx_size):
        copies.append(remote(x_ref, held.at[ctx], send.at[r], recv.at[r], ctx_peers[r - 1]))
        copies[-1].start()
    pieces = []
    for r in range(1, fsdp_size):
        pieces.append(
            remote(w_ref.at[fsdp ^ r], blocks.at[r], send3.at[r], recv3.at[r], fsdp_peers[r - 1])
        )
        pieces[-1].start()
    for copy in copies:
        copy.wait()
    total = held[0]
    for i in range(1, ctx_size):
        total = total + held[i]
    subtotal[...] = total
    others[fsdp] = total
    copies = []
    for r in range(1, fsdp_size):
        copies.append(
            remote(subtotal, others.at[fsdp], send2.at[r], recv2.at[r], fsdp_peers[r - 1])
        )
        copies[-1].start()
    for copy in pieces:
        copy.wait()
    piece = w_ref[fsdp].astype(jnp.float32)
    for r in range(1, fsdp_size):
        piece = piece + blocks[r].astype(jnp.float32)
    g_ref[...] = piece
    for copy in copies:
        copy.wait()
    total = others[0]
    for i in range(1, fsdp_size):
        total = total + others[i]
    o_ref[...] = total


def final_sum(vector, weights, collective_id):
    ctx_size = lax.axis_size("ctx")
    fsdp_size = lax.axis_size("fsdp")
    rows = vector.reshape(-1, 128)
    gains, sums = pl.pallas_call(
        functools.partial(final_body, ctx_size, fsdp_size),
        out_shape=[
            jax.ShapeDtypeStruct(rows.shape, jnp.float32),
            jax.ShapeDtypeStruct(weights.shape[1:], jnp.float32),
        ],
        in_specs=[pl.BlockSpec(memory_space=pltpu.VMEM)] * 2,
        out_specs=[pl.BlockSpec(memory_space=pltpu.VMEM)] * 2,
        scratch_shapes=[
            pltpu.VMEM((ctx_size,) + rows.shape, jnp.float32),
            pltpu.VMEM(rows.shape, jnp.float32),
            pltpu.VMEM((fsdp_size,) + rows.shape, jnp.float32),
            pltpu.VMEM(weights.shape, jnp.bfloat16),
        ]
        + [pltpu.SemaphoreType.DMA((ctx_size,))] * 2
        + [pltpu.SemaphoreType.DMA((fsdp_size,))] * 4,
        compiler_params=pltpu.CompilerParams(collective_id=collective_id, has_side_effects=True),
        name="final_sum",
    )(rows, weights)
    return gains.reshape(-1), sums


def spread(shard, axis_name):
    members = lax.axis_size(axis_name)
    copies = jnp.broadcast_to(shard[None], (members,) + shard.shape)
    return swap_blocks(copies, axis_name).reshape(members * shard.shape[0], shard.shape[1])


def swap_blocks(blocks, axis_name):
    return lax.all_to_all(blocks, axis_name, split_axis=0, concat_axis=0, tiled=True)


def scatter_sum(partial, axis_name):
    members = lax.axis_size(axis_name)
    blocks = partial.astype(jnp.bfloat16).reshape(members, -1, partial.shape[-1])
    return jnp.sum(swap_blocks(blocks, axis_name).astype(jnp.float32), axis=0)


def attention_forward(queries, key_rows, value_rows, allowed, score_scale):
    scores = (
        jnp.einsum("bshd,bnd->bshn", queries, key_rows, preferred_element_type=jnp.float32)
        * score_scale
    )
    masked = jnp.where(allowed, scores, MASK_FLOOR)
    best_score = jnp.max(masked, axis=-1)
    weights = jnp.where(allowed, jnp.exp(scores - best_score[..., None]), 0.0)
    totals = jnp.sum(weights, axis=-1)
    attended = (
        jnp.einsum(
            "bshn,bnd->bshd",
            weights,
            value_rows.astype(jnp.float32),
            precision=lax.Precision.HIGHEST,
        )
        / totals[..., None]
    )
    return (attended, best_score + jnp.log(totals))


def attention_backward(
    queries, key_rows, value_rows, allowed, score_scale, log_total, attended, attended_cot
):
    scores = (
        jnp.einsum("bshd,bnd->bshn", queries, key_rows, preferred_element_type=jnp.float32)
        * score_scale
    )
    probabilities = jnp.where(allowed, jnp.exp(scores - log_total[..., None]), 0.0)
    row_delta = jnp.sum(attended_cot.astype(jnp.float32) * attended, axis=-1)
    prob_cot = jnp.einsum(
        "bshd,bnd->bshn", attended_cot, value_rows, preferred_element_type=jnp.float32
    )
    score_cot = (probabilities * (prob_cot - row_delta[..., None])).astype(jnp.bfloat16)
    query_cot = (
        jnp.einsum("bshn,bnd->bshd", score_cot, key_rows, preferred_element_type=jnp.float32)
        * score_scale
    )
    key_cot = (
        jnp.einsum("bshn,bshd->bnd", score_cot, queries, preferred_element_type=jnp.float32)
        * score_scale
    )
    value_cot = jnp.einsum(
        "bshn,bshd->bnd",
        probabilities.astype(jnp.bfloat16),
        attended_cot,
        preferred_element_type=jnp.float32,
    )
    return (query_cot, key_cot, value_cot)


def on_device(
    block_input,
    doc_ids,
    positions,
    qkv_weight,
    out_weight,
    gate_up_weight,
    down_weight,
    scale_attn_in,
    scale_attn_out,
    scale_ff_in,
    scale_ff_out,
    scale_query,
    scale_key,
    grad_output,
):
    ctx_size = lax.axis_size("ctx")
    fsdp_size = lax.axis_size("fsdp")
    ctx_index = lax.axis_index("ctx")
    seq_count = block_input.shape[1]
    seq_rows = block_input.shape[2]
    row_count = seq_count * seq_rows
    key_count = ctx_size * seq_rows
    head_total = HEADS * HEAD_DIM
    score_scale = HEAD_DIM ** (-0.5)
    part = FF // ctx_size
    piece = part // fsdp_size
    padded = (part + 127) // 128 * 128
    (qkv_full,) = gather(("fsdp",), (qkv_weight,), 1)
    down_piece = lax.ppermute(
        lax.dynamic_slice_in_dim(down_weight, ctx_index * piece, piece, 0),
        ("ctx", "fsdp"),
        [
            (c * fsdp_size + f, (c + ctx_size * f))
            for c in range(ctx_size)
            for f in range(fsdp_size)
        ],
    )
    down_part = jnp.pad(spread(down_piece, "fsdp"), ((0, padded - part), (0, 0)))
    widen = ((0, 0), (0, padded - part))
    gate_up_w = spread(
        jnp.concatenate(
            [
                jnp.pad(lax.dynamic_slice_in_dim(gate_up_weight, first, part, 1), widen)
                for first in (ctx_index * part, FF + ctx_index * part)
            ],
            axis=1,
        ),
        "fsdp",
    )
    resid_in = block_input.reshape(row_count, D).astype(jnp.float32)
    scale_one = rms_scale(resid_in)
    attn_input = (resid_in * scale_one * scale_attn_in).astype(jnp.bfloat16)
    projected_qkv = jnp.dot(attn_input, qkv_full, preferred_element_type=jnp.float32)
    query_raw = projected_qkv[:, :head_total].reshape(row_count, HEADS, HEAD_DIM)
    key_raw = projected_qkv[:, head_total : head_total + HEAD_DIM]
    value_rows = projected_qkv[:, head_total + HEAD_DIM :].astype(jnp.bfloat16)
    query_scale = rms_scale(query_raw)
    key_scale = rms_scale(key_raw)
    local_pos = positions.reshape(seq_count, seq_rows)
    cosine, sine_part = rope_tables(local_pos.reshape(row_count))
    queries = rotate(
        query_raw * query_scale * scale_query, cosine[:, None, :], sine_part[:, None, :]
    ).astype(jnp.bfloat16)
    key_rows = rotate(key_raw * key_scale * scale_key, cosine, sine_part).astype(jnp.bfloat16)
    key_value, out_full = gather(
        ("ctx", "fsdp"), (jnp.concatenate([key_rows, value_rows], axis=1), out_weight), 2
    )
    key_value = key_value.reshape(ctx_size, seq_count, seq_rows, 2 * HEAD_DIM)
    key_value = key_value.transpose(1, 0, 2, 3).reshape(seq_count, key_count, 2 * HEAD_DIM)
    key_all = key_value[:, :, :HEAD_DIM]
    value_all = key_value[:, :, HEAD_DIM:]
    query_index = ctx_index * seq_rows + jnp.arange(seq_rows, dtype=jnp.int32)
    allowed = allowed_mask(local_pos, query_index, key_count)
    query_blocks = queries.reshape(seq_count, seq_rows, HEADS, HEAD_DIM)
    attended, log_total = attention_forward(query_blocks, key_all, value_all, allowed, score_scale)
    attended_low = attended.reshape(row_count, head_total).astype(jnp.bfloat16)
    projected = jnp.dot(attended_low, out_full, preferred_element_type=jnp.float32)
    scale_two = rms_scale(projected)
    middle = resid_in + projected * scale_two * scale_attn_out
    scale_three = rms_scale(middle)
    ff_input = (middle * scale_three * scale_ff_in).astype(jnp.bfloat16)
    (ff_all,) = gather(("ctx",), (ff_input,), 3)
    gate_up = add_product(ff_all, gate_up_w)
    gate_part = gate_up[:, :padded]
    up_part = gate_up[:, padded:]
    gelu_value, gelu_slope = gelu_parts(gate_part)
    activation = (gelu_value * up_part).astype(jnp.bfloat16)
    down_out = ctx_scatter(add_product(activation, down_part), 6)
    scale_four = rms_scale(down_out)
    block_output = (middle + down_out * scale_four * scale_ff_out).astype(jnp.bfloat16)
    cotangent = grad_output.reshape(row_count, D).astype(jnp.float32)
    ff_out_grad = jnp.sum(cotangent * down_out * scale_four, axis=0)
    down_cot = norm_back(down_out, scale_four, scale_ff_out, cotangent).astype(jnp.bfloat16)
    (down_cot_all,) = gather(("ctx",), (down_cot,), 4)
    act_cot = transposed_product(down_cot_all, down_part)
    gate_up_cot = jnp.concatenate(
        [act_cot * up_part * gelu_slope, act_cot * gelu_value], axis=1
    ).astype(jnp.bfloat16)
    ff_input_cot = ctx_scatter(transposed_product(gate_up_cot, gate_up_w), 7)
    wide_grad = transposed_left(gate_up_cot, ff_all).astype(jnp.bfloat16)
    down_partial = transposed_left(activation, down_cot_all).astype(jnp.bfloat16)
    ff_sums = scatter_sum(
        jnp.concatenate(
            [
                jnp.concatenate(
                    [wide_grad[:part], wide_grad[padded : padded + part]], axis=0
                ).reshape(fsdp_size, 2 * piece, D),
                down_partial[:part].reshape(fsdp_size, piece, D),
            ],
            axis=1,
        ),
        "fsdp",
    )
    gate_up_sum = ff_sums[: 2 * piece]
    down_grad = ff_sums[2 * piece :]
    half = fsdp_size // 2
    gate_up_grad = lax.ppermute(
        gate_up_sum,
        ("ctx", "fsdp"),
        [
            (
                c * fsdp_size + f,
                half * c + f % half + (f // half) * (ctx_size * half),
            )
            for c in range(ctx_size)
            for f in range(fsdp_size)
        ],
    ).T
    ff_in_grad = jnp.sum(ff_input_cot * middle * scale_three, axis=0)
    middle_cot = cotangent + norm_back(middle, scale_three, scale_ff_in, ff_input_cot)
    attn_out_grad = jnp.sum(middle_cot * projected * scale_two, axis=0)
    projected_cot = norm_back(projected, scale_two, scale_attn_out, middle_cot).astype(jnp.bfloat16)
    attended_cot = transposed_product(projected_cot, out_full).astype(jnp.bfloat16)
    query_cot, key_cot, value_cot = attention_backward(
        query_blocks,
        key_all,
        value_all,
        allowed,
        score_scale,
        log_total,
        attended,
        attended_cot.reshape(seq_count, seq_rows, HEADS, HEAD_DIM),
    )
    kv_partial = jnp.concatenate([key_cot, value_cot], axis=2).reshape(
        seq_count, ctx_size, seq_rows, 2 * HEAD_DIM
    )
    kv_local = ctx_scatter(kv_partial.transpose(1, 0, 2, 3), 8)
    key_cot_local = kv_local[:, :HEAD_DIM]
    value_cot_local = kv_local[:, HEAD_DIM:]
    query_back = rotate_back(
        query_cot.reshape(row_count, HEADS, HEAD_DIM), cosine[:, None, :], sine_part[:, None, :]
    )
    key_back = rotate_back(key_cot_local, cosine, sine_part)
    query_gain_grad = jnp.sum(query_back * query_raw * query_scale, axis=(0, 1))
    key_gain_grad = jnp.sum(key_back * key_raw * key_scale, axis=0)
    qkv_cot = jnp.concatenate(
        [
            norm_back(query_raw, query_scale, scale_query, query_back).reshape(
                row_count, head_total
            ),
            norm_back(key_raw, key_scale, scale_key, key_back),
            value_cot_local,
        ],
        axis=1,
    ).astype(jnp.bfloat16)
    attn_input_cot = transposed_product(qkv_cot, qkv_full)
    attn_in_grad = jnp.sum(attn_input_cot * resid_in * scale_one, axis=0)
    input_grad = middle_cot + norm_back(resid_in, scale_one, scale_attn_in, attn_input_cot)
    qkv_partial = transposed_left(qkv_cot, attn_input).astype(jnp.bfloat16)
    out_partial = transposed_left(attended_low, projected_cot).astype(jnp.bfloat16)
    weight_sums = ctx_scatter(
        jnp.concatenate(
            [qkv_partial.reshape(ctx_size, -1, D), out_partial.reshape(ctx_size, -1, D)], axis=1
        ),
        9,
    ).astype(jnp.bfloat16)
    qkv_cut = qkv_partial.shape[0] // ctx_size
    weight_blocks = jnp.concatenate(
        [
            weight_sums[:qkv_cut].reshape(fsdp_size, -1, D),
            weight_sums[qkv_cut:].reshape(fsdp_size, -1, D),
        ],
        axis=1,
    )
    gains = jnp.concatenate(
        [attn_in_grad, attn_out_grad, ff_in_grad, ff_out_grad, query_gain_grad, key_gain_grad]
    )
    gains, weight_grads = final_sum(gains, weight_blocks, 11)
    qkv_cut = qkv_cut // fsdp_size
    return (
        block_output.reshape(1, seq_count, seq_rows, D),
        input_grad.reshape(1, seq_count, seq_rows, D),
        weight_grads[:qkv_cut].T,
        weight_grads[qkv_cut:],
        gate_up_grad,
        down_grad,
        gains[:D],
        gains[D : 2 * D],
        gains[2 * D : 3 * D],
        gains[3 * D : 4 * D],
        gains[4 * D : 4 * D + HEAD_DIM],
        gains[4 * D + HEAD_DIM :],
    )


def solution(mesh):
    return jax.shard_map(
        on_device,
        mesh=mesh,
        in_specs=(
            P("fsdp", None, "ctx", None),
            P("fsdp", None, "ctx"),
            P("fsdp", None, "ctx"),
            P("fsdp", None),
            P("fsdp", None),
            P("fsdp", None),
            P("fsdp", None),
            P(),
            P(),
            P(),
            P(),
            P(),
            P(),
            P("fsdp", None, "ctx", None),
        ),
        out_specs=(
            P("fsdp", None, "ctx", None),
            P("fsdp", None, "ctx", None),
            P(None, ("ctx", "fsdp")),
            P(("ctx", "fsdp"), None),
            P(None, ("ctx", "fsdp")),
            P(("ctx", "fsdp"), None),
            P(),
            P(),
            P(),
            P(),
            P(),
            P(),
        ),
        check_vma=False,
    )
```
